256 devices in a mesh: scene: 128 (over x_lo, y, z, core), tile: 2 (over x_hi).
Axes of the slice: x: 4 (x_hi: 2, x_lo: 2; x = x_hi * 2 + x_lo), y: 4, z: 8, core: 2. Of those that a mesh axis runs over, the one named last changes fastest.
Arguments:
- features_in: bfloat16 [128, 4, 64, 4096], P('scene', 'tile'), may hold values from -6 to 6
- strided_weights: bfloat16 [2, 64, 1024], replicated, may hold values from -0.1875 to 0.1875
- dilated_weights: bfloat16 [2, 64, 576], replicated, may hold values from -0.25 to 0.25
- tile_bias: float32 [256, 64], replicated, may hold values from -3 to 3
- cost_cotangent: bfloat16 [128, 4, 1024], P('scene', 'tile'), may hold values from -6 to 6
- footprint_pairing: int32 [64, 4], replicated, may hold values from 0 to 3, each once within a row
- valid_counts: int32 [64], replicated, may hold values from 1 to 4, as said below
- tile_owner: int32 [128], replicated, may hold values from 0 to 255, as said below
Outputs:
- grad_features: bfloat16 [128, 4, 64, 4096], P('scene', 'tile')
- grad_weights: float32 [128, 1600], P('scene')
- grad_bias: float32 [256, 64], P(('scene', 'tile'))
The draws below stay inside these ranges and needn't reach their ends.
Inputs may be any that keep to these rules, and one draw needn't show every extreme that they name: `footprint_pairing`: row k maps each patch of scene 2k to the patch of scene 2k + 1 that covers its footprint; each row is a permutation. `valid_counts`: patches 0 to count - 1 of both scenes of a pair are live; some pair has all 4 live. `tile_owner`: several scenes may share a tile, and many tiles have no scene.
All inputs are finite; a program needn't handle non-finite values.
Results may differ from the reference program's by a relative error of at most 0.007.
Values may be sent and summed in bfloat16 or wider, within the bound.
A program may use at most 64 MiB of HBM per device.

```python
import math
import jax
import jax.numpy as jnp
from jax import lax

CH = 64
GRID = 64
CELLS_IN = 4096
CELLS = 1024
PATCH_SCENE = 4
SCENES = 128
PAIRS = 64
TILES = 256


def draw_valid_counts(key, part):
    first_key, second_key = jax.random.split(key)
    counts = jax.random.randint(first_key, (PAIRS,), 1, PATCH_SCENE + 1, dtype=jnp.int32)
    full_pair = jax.random.randint(second_key, (), 0, PAIRS, dtype=jnp.int32)
    return jnp.where(jnp.arange(PAIRS, dtype=jnp.int32) == full_pair, PATCH_SCENE, counts).astype(jnp.int32)


def draw_tile_owner(key, part):
    owner_key = jax.random.fold_in(key, 7)
    offset_key, bit_key, free_key = jax.random.split(owner_key, 3)
    group = TILES // SCENES
    scene_ids = jnp.arange(SCENES, dtype=jnp.int32)
    offset = jax.random.randint(offset_key, (), 0, 4, dtype=jnp.int32)
    category = (scene_ids + offset) % 4
    own_tile = scene_ids * group
    before_tile = (scene_ids - 1 + SCENES) % SCENES * group + group - 1
    far_bits = jax.random.randint(bit_key, (SCENES,), 0, group, dtype=jnp.int32)
    far_tile = (scene_ids + SCENES // 2) % SCENES * group + far_bits
    free_tile = jax.random.randint(free_key, (SCENES,), 0, TILES, dtype=jnp.int32)
    chosen = jnp.where(category == 0, own_tile, jnp.where(category == 1, before_tile, jnp.where(category == 2, far_tile, free_tile)))
    return chosen.astype(jnp.int32)


def shard_levels(stream_key, extent, cuts, smallest, high):
    def one(dim, blocks):
        draws = jax.random.uniform(jax.random.fold_in(jax.random.fold_in(stream_key, 6), dim), (blocks,), jnp.float32, smallest / len(cuts), high / len(cuts))
        return jnp.repeat(jnp.exp(draws), extent[dim] // blocks).reshape((-1,) + (1,) * (len(extent) - dim - 1))

    loudness = one(*cuts[0])
    for cut in cuts[1:]:
        loudness = loudness * one(*cut)
    return loudness


def centred(stream_key, dims, scale, limit, pieces=(), kind=jnp.bfloat16):
    values = jax.random.normal(stream_key, dims, jnp.float32) * scale
    if len(pieces) > 0:
        values = shard_levels(stream_key, dims, pieces, -0.22, 0.18) * values
    return jnp.clip(values, min=-limit, max=limit).astype(kind)


def setup_inputs(seed: int = 0) -> dict:
    key_of = jax.random.split(jax.random.key(seed), 9)
    return {
        "features_in": centred(key_of[0], (SCENES, PATCH_SCENE, CH, CELLS_IN), 1.0, 6.0, ((0, 128), (1, 2))),
        "strided_weights": centred(key_of[1], (2, CH, 16 * CH), (16 * CH) ** -0.5, 0.1875),
        "dilated_weights": centred(key_of[2], (2, CH, 9 * CH), (9 * CH) ** -0.5, 0.25),
        "tile_bias": centred(key_of[3], (TILES, CH), 0.5, 3.0, (), jnp.float32),
        "cost_cotangent": centred(key_of[4], (SCENES, PATCH_SCENE, CELLS), 1.0, 6.0, ((0, 128), (1, 2))),
        "footprint_pairing": jax.vmap(lambda own: jax.random.permutation(own, PATCH_SCENE))(jax.random.split(key_of[5], PAIRS)).reshape((PAIRS, PATCH_SCENE)).astype(jnp.int32),
        "valid_counts": draw_valid_counts(jax.random.fold_in(key_of[8], 71), 0),
        "tile_owner": draw_tile_owner(jax.random.fold_in(key_of[8], 71), 0),
    }


def strided_taps(feature_grid):
    patches, channels, grid_side = (feature_grid.shape[0], feature_grid.shape[1], feature_grid.shape[2])
    half_side = grid_side // 2
    padded = jnp.pad(feature_grid, ((0, 0), (0, 0), (1, 1), (1, 1)))
    folded = padded.reshape(patches, channels, half_side + 1, 2, half_side + 1, 2)
    tap_list = []
    for row_tap in range(4):
        for col_tap in range(4):
            row_shift, col_shift = (row_tap // 2, col_tap // 2)
            tap_piece = folded[:, :, row_shift:row_shift + half_side, row_tap % 2, col_shift:col_shift + half_side, col_tap % 2]
            tap_list.append(tap_piece.reshape(patches, channels, half_side * half_side))
    return tap_list

def strided_untaps(tap_parts, grid_side):
    patches, channels = (tap_parts[0].shape[0], tap_parts[0].shape[1])
    half_side = grid_side // 2
    tap_sums = [[jnp.zeros((patches, channels, half_side + 1, half_side + 1), jnp.float32) for col_phase in range(2)] for row_phase in range(2)]
    for row_tap in range(4):
        for col_tap in range(4):
            tap_piece = tap_parts[row_tap * 4 + col_tap].reshape(patches, channels, half_side, half_side)
            row_shift, col_shift = (row_tap // 2, col_tap // 2)
            placed = jnp.pad(tap_piece, ((0, 0), (0, 0), (row_shift, 1 - row_shift), (col_shift, 1 - col_shift)))
            tap_sums[row_tap % 2][col_tap % 2] = tap_sums[row_tap % 2][col_tap % 2] + placed
    row_stack = [jnp.stack([tap_sums[row_phase][0], tap_sums[row_phase][1]], axis=-1) for row_phase in range(2)]
    folded = jnp.stack(row_stack, axis=3)
    padded = folded.reshape(patches, channels, grid_side + 2, grid_side + 2)
    return padded[:, :, 1:grid_side + 1, 1:grid_side + 1]

def dilated_taps(feature_grid):
    patches, channels, grid_side = (feature_grid.shape[0], feature_grid.shape[1], feature_grid.shape[2])
    padded = jnp.pad(feature_grid, ((0, 0), (0, 0), (2, 2), (2, 2)))
    tap_list = []
    for row_tap in range(3):
        for col_tap in range(3):
            tap_piece = padded[:, :, 2 * row_tap:2 * row_tap + grid_side, 2 * col_tap:2 * col_tap + grid_side]
            tap_list.append(tap_piece.reshape(patches, channels, grid_side * grid_side))
    return tap_list

def dilated_untaps(tap_parts, grid_side):
    patches, channels = (tap_parts[0].shape[0], tap_parts[0].shape[1])
    running_sum = jnp.zeros((patches, channels, grid_side + 4, grid_side + 4), jnp.float32)
    for row_tap in range(3):
        for col_tap in range(3):
            tap_piece = tap_parts[row_tap * 3 + col_tap].reshape(patches, channels, grid_side, grid_side)
            running_sum = running_sum + jnp.pad(tap_piece, ((0, 0), (0, 0), (2 * row_tap, 4 - 2 * row_tap), (2 * col_tap, 4 - 2 * col_tap)))
    return running_sum[:, :, 2:grid_side + 2, 2:grid_side + 2]

def project(kernel, tap_list):
    running_sum = None
    for tap_index in range(len(tap_list)):
        tap_term = jnp.einsum('oi,pic->poc', kernel[:, :, tap_index].astype(jnp.float32), tap_list[tap_index].astype(jnp.float32))
        running_sum = tap_term if running_sum is None else running_sum + tap_term
    return running_sum

def silu_slope(pre_act):
    sigmoid_gate = jax.nn.sigmoid(pre_act)
    return sigmoid_gate * (1.0 + pre_act * (1.0 - sigmoid_gate))

def forward_block(features, strided_kernel, dilated_kernel, bias_row, grid_side):
    patches, channels = (features.shape[0], features.shape[1])
    half_side = grid_side // 2
    feature_grid = features.reshape(patches, channels, grid_side, grid_side)
    pre_act = project(strided_kernel, strided_taps(feature_grid)) + bias_row[None, :, None]
    activation = jax.nn.silu(pre_act).astype(jnp.bfloat16)
    act_grid = activation.reshape(patches, channels, half_side, half_side)
    branch_out = project(dilated_kernel, dilated_taps(act_grid)).astype(jnp.bfloat16)
    return (pre_act, activation, branch_out)

def backward_block(features, pre_act, activation, out_grad, strided_kernel, dilated_kernel, grid_side):
    patches, channels = (features.shape[0], features.shape[1])
    half_side = grid_side // 2
    out_wide = out_grad.astype(jnp.float32)
    act_list = dilated_taps(activation.reshape(patches, channels, half_side, half_side))
    grad_dilated = jnp.stack([jnp.einsum('poc,pic->oi', out_wide, tap_piece.astype(jnp.float32)) for tap_piece in act_list], axis=-1)
    act_parts = [jnp.einsum('oi,poc->pic', dilated_kernel[:, :, tap_index].astype(jnp.float32), out_wide) for tap_index in range(9)]
    act_grad = dilated_untaps(act_parts, half_side).reshape(patches, channels, half_side * half_side)
    pre_grad = act_grad * silu_slope(pre_act)
    bias_grad = lax.optimization_barrier(jnp.sum(pre_grad, axis=(0, 2)))
    pre_wide = pre_grad.astype(jnp.bfloat16).astype(jnp.float32)
    feature_list = strided_taps(features.reshape(patches, channels, grid_side, grid_side))
    grad_strided = jnp.stack([jnp.einsum('poc,pic->oi', pre_wide, tap_piece.astype(jnp.float32)) for tap_piece in feature_list], axis=-1)
    feature_parts = [jnp.einsum('oi,poc->pic', strided_kernel[:, :, tap_index].astype(jnp.float32), pre_wide) for tap_index in range(16)]
    feature_grad = strided_untaps(feature_parts, grid_side).reshape(patches, channels, grid_side * grid_side).astype(jnp.bfloat16)
    grad_row = jnp.concatenate([grad_strided.reshape(channels, channels * 16), grad_dilated.reshape(channels, channels * 9)], axis=1)
    return (grad_row, bias_grad, feature_grad)

def match_rows(pairing_row, branch, first_patch, patch_count):
    total_patches = pairing_row.shape[0]
    all_patches = jnp.arange(total_patches, dtype=jnp.int32)
    inverse = lax.optimization_barrier(jnp.sum(jnp.where(pairing_row[:, None] == all_patches[None, :], all_patches[:, None], 0), axis=0)).astype(jnp.int32)
    positions = (first_patch + jnp.arange(patch_count, dtype=jnp.int32)).astype(jnp.int32)
    return jnp.where(branch == 0, jnp.take(pairing_row, positions), jnp.take(inverse, positions)).astype(jnp.int32)

def reference(features_in, strided_weights, dilated_weights, tile_bias, cost_cotangent, footprint_pairing, valid_counts, tile_owner):
    scene_ids = jnp.arange(SCENES, dtype=jnp.int32)

    def kernels_of(scene_id):
        branch = scene_id % 2
        strided_kernel = strided_weights[branch].reshape(CH, CH, 16)
        dilated_kernel = dilated_weights[branch].reshape(CH, CH, 9)
        return (branch, strided_kernel, dilated_kernel)

    def forward_scene(scene_item):
        features, scene_id = scene_item
        branch, strided_kernel, dilated_kernel = kernels_of(scene_id)
        bias_row = tile_bias[tile_owner[scene_id]]
        return forward_block(features, strided_kernel, dilated_kernel, bias_row, GRID)
    pre_all, activation_all, branch_outs = lax.map(forward_scene, (features_in, scene_ids))

    def backward_scene(loop_state, scene_item):
        grad_rows, bias_grads = loop_state
        features, pre_act, activation, own_cotangent, scene_id = scene_item
        branch, strided_kernel, dilated_kernel = kernels_of(scene_id)
        partner = jnp.bitwise_xor(scene_id, 1).astype(jnp.int32)
        pair_index = (scene_id // 2).astype(jnp.int32)
        matched = match_rows(footprint_pairing[pair_index], branch, jnp.int32(0), PATCH_SCENE)
        partner_out = jnp.take(branch_outs[partner], matched, axis=0)
        partner_cot = jnp.take(cost_cotangent[partner], matched, axis=0)
        live_mask = (jnp.arange(PATCH_SCENE, dtype=jnp.int32) < valid_counts[pair_index]).astype(jnp.float32)
        signal = (own_cotangent.astype(jnp.float32) + partner_cot.astype(jnp.float32)) * live_mask[:, None]
        out_grad = (signal[:, None, :] * partner_out.astype(jnp.float32)).astype(jnp.bfloat16)
        grad_row, bias_grad, feature_grad = backward_block(features, pre_act, activation, out_grad, strided_kernel, dilated_kernel, GRID)
        branch_hit = jnp.arange(2, dtype=jnp.int32)[:, None, None] == branch
        grad_rows = grad_rows + jnp.where(branch_hit, grad_row[None], jnp.float32(0.0))
        tile_hit = jnp.arange(TILES, dtype=jnp.int32)[:, None] == tile_owner[scene_id]
        bias_grads = bias_grads + jnp.where(tile_hit, bias_grad[None, :], jnp.float32(0.0))
        return ((grad_rows, bias_grads), feature_grad)
    initial = (jnp.zeros((2, CH, 25 * CH), jnp.float32), jnp.zeros((TILES, CH), jnp.float32))
    (grad_rows, bias_grads), grad_features = lax.scan(backward_scene, initial, (features_in, pre_all, activation_all, cost_cotangent, scene_ids))
    weight_scale = 1.0 / math.sqrt(SCENES * PATCH_SCENE * CELLS)
    bias_scale = 1.0 / math.sqrt(PATCH_SCENE * CELLS)
    grad_weights = grad_rows.reshape(2 * CH, 25 * CH) * weight_scale
    grad_bias = bias_grads * bias_scale
    return (grad_features, grad_weights, grad_bias)
```

```python
import functools
import math

import jax
import jax.numpy as jnp
from jax import lax
from jax.experimental import pallas as pl
from jax.experimental.pallas import tpu as pltpu
from jax.sharding import PartitionSpec as P

F32 = jnp.float32
BF16 = jnp.bfloat16
MESH = pl.DeviceIdType.MESH

CH = 64
SIDE = 32
CELLS = SIDE * SIDE
GROUP = 512
GROUPS = 8
COLS = 1792
PATCHES = 2


def iota(shape, dim):
    return lax.broadcasted_iota(jnp.int32, shape, dim)


def dot(a, b):
    return lax.dot_general(a, b, (((1,), (0,)), ((), ())), preferred_element_type=F32)


def dot_nt(a, b):
    return lax.dot_general(a, b, (((1,), (1,)), ((), ())), preferred_element_type=F32)


def dot_tn(a, b):
    return lax.dot_general(a, b, (((0,), (0,)), ((), ())), preferred_element_type=F32)


def one_hot_columns(rows, target):
    cols = target.shape[1]
    hit = iota((rows, cols), 0) == target
    return jnp.where(hit, 1.0, 0.0).astype(BF16)


def column_taps():
    n = iota((1, 1024), 1)
    parity = n // 512
    tap = (n // 128) % 4
    row = (n % 128) // 32
    col = 2 * (n % 32) - 1 + tap
    target = (2 * row + parity) * 64 + col
    target = jnp.where((col >= 0) & (col < 64), target, -1)
    return one_hot_columns(GROUP, target)


def strided_order():
    n = iota((1, 1024), 1)
    return one_hot_columns(1024, (n % 64) * 16 + n // 64)


def dilated_order():
    n = iota((1, 768), 1)
    row, col, channel = n // 256, (n % 256) // 64, n % 64
    target = jnp.where(col < 3, channel * 9 + row * 3 + col, -1)
    return one_hot_columns(576, target)


def shift_rows(x, cells):
    lane = iota(x.shape, 1)
    moved = pltpu.roll(x, (-cells) % CELLS, 1)
    keep = lane < CELLS - cells if cells > 0 else lane >= -cells
    return jnp.where(keep, moved, 0.0)


def shift_cols(x, cells):
    col = iota(x.shape, 1) % SIDE
    moved = pltpu.roll(x, (-cells) % CELLS, 1)
    keep = col < SIDE - cells if cells > 0 else col >= -cells
    return jnp.where(keep, moved, 0.0)


def kernel(
    dims,
    feat,
    sw,
    dw,
    tb,
    cot,
    fp,
    vc,
    to,
    out_feat,
    out_gw,
    out_gb,
    xs,
    sel,
    perm_s,
    perm_d,
    wp,
    vp,
    taps,
    pre,
    act3,
    mine,
    theirs,
    their_cot,
    gr,
    pr,
    gw,
    acc,
    ysend,
    yrecv,
    zsend,
    zrecv,
    xsend,
    xrecv,
    bown,
    by,
    bz,
    bsend,
    brecv,
    stack,
    feat_out,
    in_sem,
    out_sem,
    ex_send,
    ex_recv,
    y_send,
    y_recv,
    z_send,
    z_recv,
    x_send,
    x_recv,
    bx_send,
    bx_recv,
):
    n_y, n_z = dims
    rows_own = CH // (2 * n_y * n_z)
    rows_z = 2 * rows_own
    rows_y = rows_z * n_z
    scene = lax.axis_index("scene")
    tile = lax.axis_index("tile")
    core = lax.rem(scene, 2)
    z = lax.rem(scene // 2, n_z)
    y = lax.rem(scene // (2 * n_z), n_y)
    x_lo = scene // (2 * n_z * n_y)
    pair = scene // 2

    def scene_of(xl, yy, zz, cc):
        return ((xl * n_y + yy) * n_z + zz) * 2 + cc

    def at_y(d):
        return lax.rem(y + d, n_y)

    def at_z(d):
        return lax.rem(z + d, n_z)

    def ring(k):
        return scene_of(k // 4, y, z, (k // 2) % 2), k % 2

    me_ring = x_lo * 4 + core * 2 + tile

    def other(k):
        return lax.rem(me_ring + k, 8)

    barrier = pltpu.get_barrier_semaphore()
    for d in range(1, n_y):
        pl.semaphore_signal(
            barrier, inc=1, device_id=(scene_of(x_lo, at_y(d), z, core), tile), device_id_type=MESH
        )
    for d in range(1, n_z):
        pl.semaphore_signal(
            barrier, inc=1, device_id=(scene_of(x_lo, y, at_z(d), core), tile), device_id_type=MESH
        )
    for k in range(1, 8):
        pl.semaphore_signal(barrier, inc=1, device_id=ring(other(k)), device_id_type=MESH)

    def load(p, h):
        return pltpu.make_async_copy(
            feat.at[0, p, :, pl.ds(h * GROUP, GROUP)], xs.at[p, h], in_sem.at[p, h]
        )

    for p in range(PATCHES):
        for h in range(GROUPS):
            load(p, h).start()

    sel[...] = column_taps()
    perm_s[...] = strided_order()
    perm_d[...] = dilated_order()
    w_all = dot(sw[core], perm_s[...]).astype(BF16)
    for slot, tap in enumerate((1, 3, 0, 2)):
        wp[slot * CH : (slot + 1) * CH, :] = w_all[:, tap * 256 : (tap + 1) * 256]
    v_all = dot(dw[core], perm_d[...]).astype(BF16)
    for tap in range(3):
        vp[tap * CH : (tap + 1) * CH, :] = v_all[:, tap * 256 : tap * 256 + 192]

    bias = jnp.sum(jnp.where(iota(tb.shape, 1) == to[scene], tb[...], 0.0), axis=1, keepdims=True)

    for p in range(PATCHES):
        for h in range(GROUPS):
            load(p, h).wait()
    for p in range(PATCHES):
        split = dot(xs[p].reshape(GROUPS * CH, GROUP), sel[...]).astype(BF16)
        for h in range(GROUPS):
            for n in range(8):
                taps[p, n * CH : (n + 1) * CH, h * 128 : (h + 1) * 128] = split[
                    h * CH : (h + 1) * CH, n * 128 : (n + 1) * 128
                ]

    def push(p, to_ring):
        return pltpu.make_async_remote_copy(
            src_ref=mine.at[p],
            dst_ref=theirs.at[tile * 2 + p],
            send_sem=ex_send.at[to_ring, p],
            recv_sem=ex_recv.at[tile, p],
            device_id=(scene_of(x_lo, y, z, 1 - core), tile if to_ring == 0 else 1 - tile),
            device_id_type=MESH,
        )

    def push_cot(to_ring):
        return pltpu.make_async_remote_copy(
            src_ref=cot.at[0],
            dst_ref=their_cot.at[tile],
            send_sem=ex_send.at[to_ring, 2],
            recv_sem=ex_recv.at[tile, 2],
            device_id=(scene_of(x_lo, y, z, 1 - core), tile if to_ring == 0 else 1 - tile),
            device_id_type=MESH,
        )

    def forward(p):
        even = dot(wp[0:128, :], taps[p, 0:256, :])
        odd = dot(wp[128:256, :], taps[p, 256:512, :])
        pre_act = (
            even[0:CH]
            + odd[CH:]
            + shift_rows(even[CH:], SIDE)
            + shift_rows(odd[0:CH], -SIDE)
            + bias
        )
        pre[p] = pre_act
        act = (pre_act * jax.nn.sigmoid(pre_act)).astype(BF16)
        wide = act.astype(F32)
        act3[p, 0:CH] = shift_cols(wide, -2).astype(BF16)
        act3[p, CH : 2 * CH] = act
        act3[p, 2 * CH :] = shift_cols(wide, 2).astype(BF16)
        rows = dot(vp[...], act3[p])
        out = (
            rows[CH : 2 * CH]
            + shift_rows(rows[0:CH], -2 * SIDE)
            + shift_rows(rows[2 * CH :], 2 * SIDE)
        )
        mine[p] = out.astype(BF16)

    forward(0)
    pl.semaphore_wait(barrier, (n_y - 1) + (n_z - 1) + 7)
    for to_ring in range(2):
        push_cot(to_ring).start()
        push(0, to_ring).start()
    forward(1)
    for to_ring in range(2):
        push(1, to_ring).start()

    def pairing(j):
        inverse = jnp.int32(0)
        for i in range(4):
            inverse = jnp.where(fp[i, pair] == j, i, inverse)
        return jnp.where(core == 0, fp[j, pair], inverse)

    live_count = vc[pair]

    for t in range(2):
        for p in range(3):
            if p < 2:
                pltpu.make_async_copy(mine.at[p], theirs.at[t * 2 + p], ex_recv.at[t, p]).wait()
            else:
                pltpu.make_async_copy(cot.at[0], their_cot.at[t], ex_recv.at[t, 2]).wait()

    bias_col = jnp.zeros((CH, 1), F32)
    for p in range(PATCHES):
        j = tile * PATCHES + p
        matched = pairing(j)
        partner_cot = jnp.zeros((1, CELLS), F32)
        for t in range(2):
            both = their_cot[t].astype(F32)
            for i in range(2):
                partner_cot = partner_cot + jnp.where(matched == t * 2 + i, both[i : i + 1], 0.0)
        own_cot = cot[0].astype(F32)[p : p + 1]
        live = jnp.where(j < live_count, 1.0, 0.0).astype(F32)
        signal = (own_cot + partner_cot) * live
        out_grad = (signal * theirs[matched].astype(F32)).astype(BF16)
        wide = out_grad.astype(F32)
        gr[0:CH] = shift_rows(wide, 2 * SIDE).astype(BF16)
        gr[CH : 2 * CH] = out_grad
        gr[2 * CH :] = shift_rows(wide, -2 * SIDE).astype(BF16)
        gdil = dot_nt(gr[...], act3[p])
        cols = dot_tn(vp[...], gr[...])
        act_grad = (
            cols[CH : 2 * CH] + shift_cols(cols[0:CH], 2) + shift_cols(cols[2 * CH :], -2)
        )
        v = pre[p]
        g = jax.nn.sigmoid(v)
        pre_grad = act_grad * (g * (1.0 + v * (1.0 - g)))
        bias_col = bias_col + jnp.sum(pre_grad, axis=1, keepdims=True)
        narrow = pre_grad.astype(BF16)
        wide = narrow.astype(F32)
        pr[p, 0:CH] = narrow
        pr[p, CH : 2 * CH] = shift_rows(wide, -SIDE).astype(BF16)
        pr[p, 2 * CH : 3 * CH] = shift_rows(wide, SIDE).astype(BF16)
        pr[p, 3 * CH :] = narrow
        geven = dot_nt(pr[p, 0:128], taps[p, 0:256])
        godd = dot_nt(pr[p, 128:256], taps[p, 256:512])
        for slot, tap in enumerate((1, 3, 0, 2)):
            part = (geven if slot < 2 else godd)[(slot % 2) * CH : (slot % 2 + 1) * CH]
            where = slice(tap * 256, (tap + 1) * 256)
            if p == 0:
                gw[:, where] = part
            else:
                gw[:, where] += part
        for tap in range(3):
            part = gdil[tap * CH : (tap + 1) * CH]
            where = slice(1024 + tap * 256, 1024 + tap * 256 + 192)
            if p == 0:
                gw[:, where] = part
                gw[:, 1024 + tap * 256 + 192 : 1024 + (tap + 1) * 256] = jnp.zeros((CH, 64), F32)
            else:
                gw[:, where] += part

    ysend[...] = gw[...].astype(BF16)
    wide_eye = iota((CH, 128), 0) == iota((CH, 128), 1)
    bown[...] = jnp.sum(
        jnp.where(wide_eye, jnp.broadcast_to(bias_col, (CH, 128)), 0.0), axis=0, keepdims=True
    )

    def y_copy(d):
        return pltpu.make_async_remote_copy(
            src_ref=ysend.at[pl.ds(pl.multiple_of(at_y(d) * rows_y, rows_y), rows_y), :],
            dst_ref=yrecv.at[y],
            send_sem=y_send.at[0, d],
            recv_sem=y_recv.at[0, y],
            device_id=(scene_of(x_lo, at_y(d), z, core), tile),
            device_id_type=MESH,
        )

    def by_copy(d):
        return pltpu.make_async_remote_copy(
            src_ref=bown,
            dst_ref=by.at[y],
            send_sem=y_send.at[1, d],
            recv_sem=y_recv.at[1, y],
            device_id=(scene_of(x_lo, at_y(d), z, core), tile),
            device_id_type=MESH,
        )

    for d in range(1, n_y):
        y_copy(d).start()
        by_copy(d).start()

    def store(p):
        return pltpu.make_async_copy(feat_out.at[p], out_feat.at[0, p], out_sem.at[p])

    def feature_grad(p):
        for half in range(2):
            part = dot_tn(
                wp[half * 128 : (half + 1) * 128, :], pr[p, half * 128 : (half + 1) * 128, :]
            ).astype(BF16)
            for h in range(GROUPS):
                for n in range(4):
                    stack[h * CH : (h + 1) * CH, (half * 4 + n) * 128 : (half * 4 + n + 1) * 128] = (
                        part[n * CH : (n + 1) * CH, h * 128 : (h + 1) * 128]
                    )
        whole = dot_nt(stack[...], sel[...]).astype(BF16)
        for h in range(GROUPS):
            feat_out[p, :, h * GROUP : (h + 1) * GROUP] = whole[h * CH : (h + 1) * CH]
        store(p).start()

    feature_grad(0)

    by[pl.ds(y, 1)] = bown[...][None]
    total = gw[pl.ds(pl.multiple_of(y * rows_y, rows_y), rows_y), :]
    for d in range(1, n_y):
        source = at_y(d)
        pltpu.make_async_copy(ysend.at[0:rows_y, :], yrecv.at[source], y_recv.at[0, source]).wait()
        total = total + yrecv[source].astype(F32)
    for d in range(1, n_y):
        source = at_y(d)
        pltpu.make_async_copy(bown, by.at[source], y_recv.at[1, source]).wait()
    for k in range(n_z):
        zsend[k] = total[k * rows_z : (k + 1) * rows_z]

    def z_copy(d):
        return pltpu.make_async_remote_copy(
            src_ref=zsend.at[at_z(d)],
            dst_ref=zrecv.at[z],
            send_sem=z_send.at[0, d],
            recv_sem=z_recv.at[0, z],
            device_id=(scene_of(x_lo, y, at_z(d), core), tile),
            device_id_type=MESH,
        )

    def bz_copy(d):
        return pltpu.make_async_remote_copy(
            src_ref=by,
            dst_ref=bz.at[z],
            send_sem=z_send.at[1, d],
            recv_sem=z_recv.at[1, z],
            device_id=(scene_of(x_lo, y, at_z(d), core), tile),
            device_id_type=MESH,
        )

    for d in range(1, n_z):
        z_copy(d).start()
        bz_copy(d).start()

    feature_grad(1)

    total = zsend[z]
    for d in range(1, n_z):
        source = at_z(d)
        pltpu.make_async_copy(zsend.at[0], zrecv.at[source], z_recv.at[0, source]).wait()
        total = total + zrecv[source]
    bz[pl.ds(z, 1)] = by[...][None]
    for d in range(1, n_z):
        source = at_z(d)
        pltpu.make_async_copy(by, bz.at[source], z_recv.at[1, source]).wait()
    for r in range(2):
        xsend[r] = total[r * rows_own : (r + 1) * rows_own]

    k8 = iota((8, 128), 0)
    tile_ids = scene_of(k8 // 4, y, z, (k8 // 2) % 2) * 2 + k8 % 2
    sums = jnp.zeros((8, 128), F32)
    for zz in range(n_z):
        for yy in range(n_y):
            owner = to[scene_of(x_lo, yy, zz, core)]
            sums = sums + jnp.where(tile_ids == owner, bz[zz, yy], 0.0)
    for k in range(8):
        bsend[k] = sums[k : k + 1]

    here = tile * 2 + x_lo

    def x_copy(r, t):
        return pltpu.make_async_remote_copy(
            src_ref=xsend.at[r],
            dst_ref=xrecv.at[here],
            send_sem=x_send.at[r, t],
            recv_sem=x_recv.at[here],
            device_id=(scene_of(core, y, z, r), t),
            device_id_type=MESH,
        )

    def is_me(r, t):
        return (x_lo == core) & (core == r) & (tile == t)

    def bx_copy(k):
        return pltpu.make_async_remote_copy(
            src_ref=bsend.at[other(k)],
            dst_ref=brecv.at[me_ring],
            send_sem=bx_send.at[k],
            recv_sem=bx_recv.at[me_ring],
            device_id=ring(other(k)),
            device_id_type=MESH,
        )

    for r in range(2):
        for t in range(2):

            @pl.when(jnp.logical_not(is_me(r, t)))
            def _():
                x_copy(r, t).start()

            @pl.when(is_me(r, t))
            def _():
                xrecv[pl.ds(here, 1)] = xsend[r][None]

    for k in range(1, 8):
        bx_copy(k).start()

    brecv[pl.ds(me_ring, 1)] = bsend[pl.ds(me_ring, 1)]
    for s in range(4):

        @pl.when(jnp.logical_not((core == x_lo) & (here == s)))
        def _():
            pltpu.make_async_copy(xsend.at[0], xrecv.at[s], x_recv.at[s]).wait()

    scale = 1.0 / math.sqrt(4 * n_y * n_z * PATCHES * 2 * CELLS)
    rows = (xrecv[0] + xrecv[1] + xrecv[2] + xrecv[3]) * scale
    sub = iota((16, COLS), 0)
    for r in range(rows_own):
        row = rows[r : r + 1]
        high = row.astype(BF16).astype(F32)
        rest = row - high
        middle = rest.astype(BF16).astype(F32)
        low = rest - middle
        parts = jnp.where(
            sub == 0, high, jnp.where(sub == 1, middle, jnp.where(sub == 2, low, 0.0))
        ).astype(BF16)
        strided = dot_nt(parts[:, 0:1024], perm_s[...])
        dilated = dot_nt(parts[:, 1024:], perm_d[...])
        out_gw[r : r + 1, 0:1024] = jnp.sum(strided, axis=0, keepdims=True)
        out_gw[r : r + 1, 1024:1600] = jnp.sum(dilated, axis=0, keepdims=True)

    for k in range(1, 8):
        source = other(k)
        pltpu.make_async_copy(bsend.at[0], brecv.at[source], bx_recv.at[source]).wait()
    bias_total = brecv[0]
    for k in range(1, 8):
        bias_total = bias_total + brecv[k]
    bias_scale = 1.0 / math.sqrt(2 * PATCHES * CELLS)
    out_gb[...] = bias_total[:, 0:CH] * bias_scale

    for p in range(PATCHES):
        store(p).wait()
    for to_ring in range(2):
        push_cot(to_ring).wait_send()
        for p in range(PATCHES):
            push(p, to_ring).wait_send()
    for d in range(1, n_y):
        y_copy(d).wait_send()
        by_copy(d).wait_send()
    for d in range(1, n_z):
        z_copy(d).wait_send()
        bz_copy(d).wait_send()
    for r in range(2):
        for t in range(2):

            @pl.when(jnp.logical_not(is_me(r, t)))
            def _():
                x_copy(r, t).wait_send()

    for k in range(1, 8):
        bx_copy(k).wait_send()


def grid_of(scenes):
    n_z = 8 if scenes == 128 else 1
    return scenes // (4 * n_z), n_z


def local(dims, features_in, sw, dw, tb, cot, fp, vc, to):
    n_y, n_z = dims
    rows_own = CH // (2 * n_y * n_z)
    rows_y = 2 * rows_own * n_z
    vmem = pl.BlockSpec(memory_space=pltpu.VMEM)
    smem = pl.BlockSpec(memory_space=pltpu.SMEM)
    anywhere = pl.BlockSpec(memory_space=pl.ANY)
    dma = pltpu.SemaphoreType.DMA
    V = pltpu.VMEM
    return pl.pallas_call(
        functools.partial(kernel, dims),
        out_shape=(
            jax.ShapeDtypeStruct(features_in.shape, BF16),
            jax.ShapeDtypeStruct((rows_own, 1600), F32),
            jax.ShapeDtypeStruct((1, CH), F32),
        ),
        in_specs=[anywhere, vmem, vmem, vmem, vmem, smem, smem, smem],
        out_specs=(anywhere, vmem, vmem),
        scratch_shapes=[
            V((PATCHES, GROUPS, CH, GROUP), BF16),
            V((GROUP, 1024), BF16),
            V((1024, 1024), BF16),
            V((576, 768), BF16),
            V((256, 256), BF16),
            V((192, 192), BF16),
            V((PATCHES, 512, CELLS), BF16),
            V((PATCHES, CH, CELLS), F32),
            V((PATCHES, 192, CELLS), BF16),
            V((PATCHES, CH, CELLS), BF16),
            V((4, CH, CELLS), BF16),
            V((2, 2, CELLS), BF16),
            V((192, CELLS), BF16),
            V((PATCHES, 256, CELLS), BF16),
            V((CH, COLS), F32),
            V((8, 128), F32),
            V((CH, COLS), BF16),
            V((n_y, rows_y, COLS), BF16),
            V((n_z, 2 * rows_own, COLS), F32),
            V((n_z, 2 * rows_own, COLS), F32),
            V((2, rows_own, COLS), F32),
            V((4, rows_own, COLS), F32),
            V((1, 128), F32),
            V((n_y, 1, 128), F32),
            V((n_z, n_y, 1, 128), F32),
            V((8, 1, 128), F32),
            V((8, 1, 128), F32),
            V((GROUPS * CH, 1024), BF16),
            V((PATCHES, CH, 4096), BF16),
            dma((PATCHES, GROUPS)),
            dma((PATCHES,)),
            dma((2, 3)),
            dma((2, 3)),
            dma((2, n_y)),
            dma((2, n_y)),
            dma((2, n_z)),
            dma((2, n_z)),
            dma((2, 2)),
            dma((4,)),
            dma((8,)),
            dma((8,)),
        ],
        compiler_params=pltpu.CompilerParams(
            collective_id=0, has_side_effects=True, vmem_limit_bytes=60 * 1024 * 1024
        ),
    )(features_in, sw, dw, tb.T, cot, fp.T, vc, to)


def solution(mesh):
    return jax.shard_map(
        functools.partial(local, grid_of(mesh.shape["scene"])),
        mesh=mesh,
        in_specs=(
            P("scene", "tile", None, None),
            P(),
            P(),
            P(),
            P("scene", "tile", None),
            P(),
            P(),
            P(),
        ),
        out_specs=(P("scene", "tile", None, None), P("scene", None), P(("scene", "tile"), None)),
        check_vma=False,
    )
```

```python
import functools
import math

import jax
import jax.numpy as jnp
from jax import lax
from jax.experimental import pallas as pl
from jax.experimental.pallas import tpu as pltpu
from jax.sharding import PartitionSpec as P

F32 = jnp.float32
BF16 = jnp.bfloat16
MESH = pl.DeviceIdType.MESH

CH = 64
SIDE = 32
CELLS = SIDE * SIDE
GROUP = 512
GROUPS = 8
COLS = (768, 1024)
PATCHES = 2


def iota(shape, dim):
    return lax.broadcasted_iota(jnp.int32, shape, dim)


def dot(a, b):
    return lax.dot_general(a, b, (((1,), (0,)), ((), ())), preferred_element_type=F32)


def dot_nt(a, b):
    return lax.dot_general(a, b, (((1,), (1,)), ((), ())), preferred_element_type=F32)


def dot_tn(a, b):
    return lax.dot_general(a, b, (((0,), (0,)), ((), ())), preferred_element_type=F32)


def one_hot_columns(rows, target):
    cols = target.shape[1]
    hit = iota((rows, cols), 0) == target
    return jnp.where(hit, 1.0, 0.0).astype(BF16)


def column_taps():
    n = iota((1, 1024), 1)
    parity = n // 512
    tap = (n // 128) % 4
    row = (n % 128) // 32
    col = 2 * (n % 32) - 1 + tap
    target = (2 * row + parity) * 64 + col
    target = jnp.where((col >= 0) & (col < 64), target, -1)
    return one_hot_columns(GROUP, target)


def strided_order():
    n = iota((1, 1024), 1)
    return one_hot_columns(1024, (n % 64) * 16 + n // 64)


def dilated_order():
    n = iota((1, 768), 1)
    row, col, channel = n // 256, (n % 256) // 64, n % 64
    target = jnp.where(col < 3, channel * 9 + row * 3 + col, -1)
    return one_hot_columns(576, target)


def shift_rows(x, cells):
    lane = iota(x.shape, 1)
    moved = pltpu.roll(x, (-cells) % CELLS, 1)
    keep = lane < CELLS - cells if cells > 0 else lane >= -cells
    return jnp.where(keep, moved, 0.0)


def shift_cols(x, cells):
    col = iota(x.shape, 1) % SIDE
    moved = pltpu.roll(x, (-cells) % CELLS, 1)
    keep = col < SIDE - cells if cells > 0 else col >= -cells
    return jnp.where(keep, moved, 0.0)


def kernel(
    dims,
    feat,
    sw_in,
    dw_in,
    tb_in,
    cot_in,
    fp_in,
    vc_in,
    to_in,
    out_feat,
    out_a,
    out_b,
    out_bias,
    sw,
    dw,
    tb,
    cot,
    fp,
    vc,
    to,
    xs,
    sel,
    perm_s,
    perm_d,
    wp,
    vp,
    taps,
    pre,
    act3,
    mine,
    theirs,
    their_cot,
    gr,
    pr,
    gw_a,
    gw_b,
    ysend_a,
    ysend_b,
    yrecv_a,
    yrecv_b,
    zsend_a,
    zsend_b,
    zrecv_a,
    zrecv_b,
    xsend_a,
    xsend_b,
    xrecv_a,
    xrecv_b,
    bown,
    by,
    bz,
    bsend,
    brecv,
    stack,
    feat_out,
    w_sem,
    in_sem,
    out_sem,
    ex_send,
    ex_recv,
    y_send,
    y_recv,
    z_send,
    z_recv,
    x_send,
    x_recv,
    bx_send,
    bx_recv,
):
    n_y, n_z = dims
    rows_own = CH // (2 * n_y * n_z)
    rows_z = 2 * rows_own
    rows_y = rows_z * n_z
    gw = (gw_a, gw_b)
    ysend = (ysend_a, ysend_b)
    yrecv = (yrecv_a, yrecv_b)
    zsend = (zsend_a, zsend_b)
    zrecv = (zrecv_a, zrecv_b)
    xsend = (xsend_a, xsend_b)
    xrecv = (xrecv_a, xrecv_b)
    scene = lax.axis_index("scene")
    tile = lax.axis_index("tile")
    core = lax.rem(scene, 2)
    z = lax.rem(scene // 2, n_z)
    y = lax.rem(scene // (2 * n_z), n_y)
    x_lo = scene // (2 * n_z * n_y)
    pair = scene // 2

    def scene_of(xl, yy, zz, cc):
        return ((xl * n_y + yy) * n_z + zz) * 2 + cc

    def at_y(d):
        return lax.rem(y + d, n_y)

    def at_z(d):
        return lax.rem(z + d, n_z)

    def ring(k):
        return scene_of(k // 4, y, z, (k // 2) % 2), k % 2

    me_ring = x_lo * 4 + core * 2 + tile

    def other(k):
        return lax.rem(me_ring + k, 8)

    def load(p, h):
        return pltpu.make_async_copy(
            feat.at[0, p, :, pl.ds(h * GROUP, GROUP)], xs.at[p, h], in_sem.at[p, h]
        )

    def load_small(i):
        source, target = (
            (sw_in.at[core], sw),
            (dw_in.at[core], dw),
            (tb_in, tb),
            (cot_in.at[0], cot),
            (fp_in, fp),
            (vc_in, vc),
            (to_in, to),
        )[i]
        return pltpu.make_async_copy(source, target, w_sem.at[i])

    load_small(0).start()
    load_small(1).start()
    for h in range(GROUPS):
        load(0, h).start()
    for i in range(2, 7):
        load_small(i).start()
    for h in range(GROUPS):
        load(1, h).start()

    barrier = pltpu.get_barrier_semaphore()
    for d in range(1, n_y):
        pl.semaphore_signal(
            barrier, inc=1, device_id=(scene_of(x_lo, at_y(d), z, core), tile), device_id_type=MESH
        )
    for d in range(1, n_z):
        pl.semaphore_signal(
            barrier, inc=1, device_id=(scene_of(x_lo, y, at_z(d), core), tile), device_id_type=MESH
        )
    for k in range(1, 8):
        pl.semaphore_signal(barrier, inc=1, device_id=ring(other(k)), device_id_type=MESH)

    sel[...] = column_taps()
    perm_s[...] = strided_order()
    perm_d[...] = dilated_order()
    load_small(0).wait()
    w_all = dot(sw[...], perm_s[...]).astype(BF16)
    for slot, tap in enumerate((1, 3, 0, 2)):
        wp[slot * CH : (slot + 1) * CH, :] = w_all[:, tap * 256 : (tap + 1) * 256]
    load_small(1).wait()
    v_all = dot(dw[...], perm_d[...]).astype(BF16)
    for tap in range(3):
        vp[tap * CH : (tap + 1) * CH, :] = v_all[:, tap * 256 : tap * 256 + 192]
    for i in range(2, 7):
        load_small(i).wait()
    bias = jnp.sum(jnp.where(iota(tb.shape, 1) == to[scene], tb[...], 0.0), axis=1, keepdims=True)

    def split(p):
        for h in range(GROUPS):
            load(p, h).wait()
        parts = dot(xs[p].reshape(GROUPS * CH, GROUP), sel[...]).astype(BF16)
        for h in range(GROUPS):
            for n in range(8):
                taps[p, n * CH : (n + 1) * CH, h * 128 : (h + 1) * 128] = parts[
                    h * CH : (h + 1) * CH, n * 128 : (n + 1) * 128
                ]

    def partner(to_ring):
        return scene_of(x_lo, y, z, 1 - core), tile if to_ring == 0 else 1 - tile

    def push(p, to_ring):
        return pltpu.make_async_remote_copy(
            src_ref=mine.at[p],
            dst_ref=theirs.at[tile * 2 + p],
            send_sem=ex_send.at[to_ring, p],
            recv_sem=ex_recv.at[tile, p],
            device_id=partner(to_ring),
            device_id_type=MESH,
        )

    def push_cot(to_ring):
        return pltpu.make_async_remote_copy(
            src_ref=cot,
            dst_ref=their_cot.at[tile],
            send_sem=ex_send.at[to_ring, 2],
            recv_sem=ex_recv.at[tile, 2],
            device_id=partner(to_ring),
            device_id_type=MESH,
        )

    def forward(p):
        even = dot(wp[0:128, :], taps[p, 0:256, :])
        odd = dot(wp[128:256, :], taps[p, 256:512, :])
        pre_act = (
            even[0:CH]
            + odd[CH:]
            + shift_rows(even[CH:], SIDE)
            + shift_rows(odd[0:CH], -SIDE)
            + bias
        )
        pre[p] = pre_act
        act = (pre_act * jax.nn.sigmoid(pre_act)).astype(BF16)
        wide = act.astype(F32)
        act3[p, 0:CH] = shift_cols(wide, -2).astype(BF16)
        act3[p, CH : 2 * CH] = act
        act3[p, 2 * CH :] = shift_cols(wide, 2).astype(BF16)
        rows = dot(vp[...], act3[p])
        out = (
            rows[CH : 2 * CH]
            + shift_rows(rows[0:CH], -2 * SIDE)
            + shift_rows(rows[2 * CH :], 2 * SIDE)
        )
        mine[p] = out.astype(BF16)

    for p in range(PATCHES):
        split(p)
        forward(p)
        if p == 0:
            pl.semaphore_wait(barrier, (n_y - 1) + (n_z - 1) + 7)
        for to_ring in (1, 0):
            push(p, to_ring).start()
            if p == 0:
                push_cot(to_ring).start()

    for p in range(PATCHES):
        v = pre[p]
        g = jax.nn.sigmoid(v)
        pre[p] = g * (1.0 + v * (1.0 - g))

    def pairing(j):
        inverse = jnp.int32(0)
        for i in range(4):
            inverse = jnp.where(fp[i, pair] == j, i, inverse)
        return jnp.where(core == 0, fp[j, pair], inverse)

    live_count = vc[pair]

    for t in range(2):
        for p in range(3):
            if p < 2:
                pltpu.make_async_copy(mine.at[p], theirs.at[t * 2 + p], ex_recv.at[t, p]).wait()
            else:
                pltpu.make_async_copy(cot, their_cot.at[t], ex_recv.at[t, 2]).wait()

    def y_copy(c, d):
        return pltpu.make_async_remote_copy(
            src_ref=ysend[c].at[pl.ds(pl.multiple_of(at_y(d) * rows_y, rows_y), rows_y), :],
            dst_ref=yrecv[c].at[y],
            send_sem=y_send.at[c, d],
            recv_sem=y_recv.at[c, y],
            device_id=(scene_of(x_lo, at_y(d), z, core), tile),
            device_id_type=MESH,
        )

    def by_copy(d):
        return pltpu.make_async_remote_copy(
            src_ref=bown,
            dst_ref=by.at[y],
            send_sem=y_send.at[2, d],
            recv_sem=y_recv.at[2, y],
            device_id=(scene_of(x_lo, at_y(d), z, core), tile),
            device_id_type=MESH,
        )

    def z_copy(c, d):
        return pltpu.make_async_remote_copy(
            src_ref=zsend[c].at[at_z(d)],
            dst_ref=zrecv[c].at[z],
            send_sem=z_send.at[c, d],
            recv_sem=z_recv.at[c, z],
            device_id=(scene_of(x_lo, y, at_z(d), core), tile),
            device_id_type=MESH,
        )

    def bz_copy(d):
        return pltpu.make_async_remote_copy(
            src_ref=by,
            dst_ref=bz.at[z],
            send_sem=z_send.at[2, d],
            recv_sem=z_recv.at[2, z],
            device_id=(scene_of(x_lo, y, at_z(d), core), tile),
            device_id_type=MESH,
        )

    here = tile * 2 + x_lo

    def x_copy(c, r, t):
        return pltpu.make_async_remote_copy(
            src_ref=xsend[c].at[r],
            dst_ref=xrecv[c].at[here],
            send_sem=x_send.at[c, r, t],
            recv_sem=x_recv.at[c, here],
            device_id=(scene_of(core, y, z, r), t),
            device_id_type=MESH,
        )

    def is_me(r, t):
        return (x_lo == core) & (core == r) & (tile == t)

    def bx_copy(k):
        return pltpu.make_async_remote_copy(
            src_ref=bsend.at[other(k)],
            dst_ref=brecv.at[me_ring],
            send_sem=bx_send.at[k],
            recv_sem=bx_recv.at[me_ring],
            device_id=ring(other(k)),
            device_id_type=MESH,
        )

    def start_y(c):
        ysend[c][...] = gw[c][...].astype(BF16)
        for d in range(n_y - 1, 0, -1):
            y_copy(c, d).start()

    def y_to_z(c):
        total = gw[c][pl.ds(pl.multiple_of(y * rows_y, rows_y), rows_y), :]
        for d in range(1, n_y):
            source = at_y(d)
            pltpu.make_async_copy(
                ysend[c].at[0:rows_y, :], yrecv[c].at[source], y_recv.at[c, source]
            ).wait()
            total = total + yrecv[c][source].astype(F32)
        for k in range(n_z):
            zsend[c][k] = total[k * rows_z : (k + 1) * rows_z].astype(BF16)
        for d in range(1, n_z):
            z_copy(c, d).start()

    def z_to_x(c):
        total = zsend[c][z].astype(F32)
        for d in range(1, n_z):
            source = at_z(d)
            pltpu.make_async_copy(zsend[c].at[0], zrecv[c].at[source], z_recv.at[c, source]).wait()
            total = total + zrecv[c][source].astype(F32)
        for r in range(2):
            xsend[c][r] = total[r * rows_own : (r + 1) * rows_own]
        for r in range(2):
            for t in range(2):

                @pl.when(jnp.logical_not(is_me(r, t)))
                def _():
                    x_copy(c, r, t).start()

                @pl.when(is_me(r, t))
                def _():
                    xrecv[c][pl.ds(here, 1)] = xsend[c][r][None]

    def x_done(c, out):
        for s in range(4):

            @pl.when(jnp.logical_not((core == x_lo) & (here == s)))
            def _():
                pltpu.make_async_copy(xsend[c].at[0], xrecv[c].at[s], x_recv.at[c, s]).wait()

        out[...] = xrecv[c][0] + xrecv[c][1] + xrecv[c][2] + xrecv[c][3]

    for p in range(PATCHES):
        j = tile * PATCHES + p
        matched = pairing(j)
        partner_cot = jnp.zeros((1, CELLS), F32)
        for t in range(2):
            both = their_cot[t].astype(F32)
            for i in range(2):
                partner_cot = partner_cot + jnp.where(matched == t * 2 + i, both[i : i + 1], 0.0)
        own_cot = cot[...].astype(F32)[p : p + 1]
        live = jnp.where(j < live_count, 1.0, 0.0).astype(F32)
        signal = (own_cot + partner_cot) * live
        out_grad = (signal * theirs[matched].astype(F32)).astype(BF16)
        wide = out_grad.astype(F32)
        gr[p, 0:CH] = shift_rows(wide, 2 * SIDE).astype(BF16)
        gr[p, CH : 2 * CH] = out_grad
        gr[p, 2 * CH :] = shift_rows(wide, -2 * SIDE).astype(BF16)
        gdil = dot_nt(gr[p], act3[p])
        for tap in range(3):
            part = gdil[tap * CH : (tap + 1) * CH]
            where = slice(tap * 256, tap * 256 + 192)
            if p == 0:
                gw_a[:, where] = part
                gw_a[:, tap * 256 + 192 : (tap + 1) * 256] = jnp.zeros((CH, 64), F32)
            else:
                gw_a[:, where] += part
    start_y(0)

    bias_col = jnp.zeros((CH, 1), F32)
    for p in range(PATCHES):
        cols = dot_tn(vp[...], gr[p])
        act_grad = (
            cols[CH : 2 * CH] + shift_cols(cols[0:CH], 2) + shift_cols(cols[2 * CH :], -2)
        )
        pre_grad = act_grad * pre[p]
        bias_col = bias_col + jnp.sum(pre_grad, axis=1, keepdims=True)
        narrow = pre_grad.astype(BF16)
        wide = narrow.astype(F32)
        pr[p, 0:CH] = narrow
        pr[p, CH : 2 * CH] = shift_rows(wide, -SIDE).astype(BF16)
        pr[p, 2 * CH : 3 * CH] = shift_rows(wide, SIDE).astype(BF16)
        pr[p, 3 * CH :] = narrow
        geven = dot_nt(pr[p, 0:128], taps[p, 0:256])
        godd = dot_nt(pr[p, 128:256], taps[p, 256:512])
        for slot, tap in enumerate((1, 3, 0, 2)):
            part = (geven if slot < 2 else godd)[(slot % 2) * CH : (slot % 2 + 1) * CH]
            where = slice(tap * 256, (tap + 1) * 256)
            if p == 0:
                gw_b[:, where] = part
            else:
                gw_b[:, where] += part
    start_y(1)

    wide_eye = iota((CH, 128), 0) == iota((CH, 128), 1)
    bown[...] = jnp.sum(
        jnp.where(wide_eye, jnp.broadcast_to(bias_col, (CH, 128)), 0.0), axis=0, keepdims=True
    )
    for d in range(1, n_y):
        by_copy(d).start()
    by[pl.ds(y, 1)] = bown[...][None]

    def store(p):
        return pltpu.make_async_copy(feat_out.at[p], out_feat.at[0, p], out_sem.at[p])

    def feature_grad(p):
        for half in range(2):
            part = dot_tn(
                wp[half * 128 : (half + 1) * 128, :], pr[p, half * 128 : (half + 1) * 128, :]
            ).astype(BF16)
            for h in range(GROUPS):
                for n in range(4):
                    stack[h * CH : (h + 1) * CH, (half * 4 + n) * 128 : (half * 4 + n + 1) * 128] = (
                        part[n * CH : (n + 1) * CH, h * 128 : (h + 1) * 128]
                    )
        whole = dot_nt(stack[...], sel[...]).astype(BF16)
        for h in range(GROUPS):
            feat_out[p, :, h * GROUP : (h + 1) * GROUP] = whole[h * CH : (h + 1) * CH]
        store(p).start()

    feature_grad(0)
    y_to_z(0)
    feature_grad(1)
    y_to_z(1)
    for d in range(1, n_y):
        source = at_y(d)
        pltpu.make_async_copy(bown, by.at[source], y_recv.at[2, source]).wait()
    for d in range(1, n_z):
        bz_copy(d).start()
    z_to_x(0)
    z_to_x(1)

    bz[pl.ds(z, 1)] = by[...][None]
    for d in range(1, n_z):
        source = at_z(d)
        pltpu.make_async_copy(by, bz.at[source], z_recv.at[2, source]).wait()
    k8 = iota((8, 128), 0)
    tile_ids = scene_of(k8 // 4, y, z, (k8 // 2) % 2) * 2 + k8 % 2
    sums = jnp.zeros((8, 128), F32)
    for zz in range(n_z):
        for yy in range(n_y):
            owner = to[scene_of(x_lo, yy, zz, core)]
            sums = sums + jnp.where(tile_ids == owner, bz[zz, yy], 0.0)
    for k in range(8):
        bsend[k] = sums[k : k + 1]
    for k in range(1, 8):
        bx_copy(k).start()
    brecv[pl.ds(me_ring, 1)] = bsend[pl.ds(me_ring, 1)]

    x_done(0, out_a)
    x_done(1, out_b)
    for k in range(1, 8):
        source = other(k)
        pltpu.make_async_copy(bsend.at[0], brecv.at[source], bx_recv.at[source]).wait()
    bias_total = brecv[0]
    for k in range(1, 8):
        bias_total = bias_total + brecv[k]
    out_bias[...] = bias_total

    for p in range(PATCHES):
        store(p).wait()
    for to_ring in range(2):
        push_cot(to_ring).wait_send()
        for p in range(PATCHES):
            push(p, to_ring).wait_send()
    for d in range(1, n_y):
        for c in range(2):
            y_copy(c, d).wait_send()
        by_copy(d).wait_send()
    for d in range(1, n_z):
        for c in range(2):
            z_copy(c, d).wait_send()
        bz_copy(d).wait_send()
    for c in range(2):
        for r in range(2):
            for t in range(2):

                @pl.when(jnp.logical_not(is_me(r, t)))
                def _():
                    x_copy(c, r, t).wait_send()

    for k in range(1, 8):
        bx_copy(k).wait_send()


def pick(row, vregs, out_cols, taps, slot_of):
    split = jnp.concatenate([row[:, q * 128 : (q + 1) * 128] for q in range(vregs)], axis=0)
    if vregs < 8:
        split = jnp.concatenate([split, jnp.zeros((8 - vregs, 128), F32)], axis=0)
    high = split.astype(BF16).astype(F32)
    rest = split - high
    middle = rest.astype(BF16).astype(F32)
    low = rest - middle
    parts = jnp.concatenate([high, middle, low], axis=0).astype(BF16)
    lane = iota((1, out_cols), 1)
    slot = slot_of(lane % taps)
    sub = iota((8, out_cols), 0)
    total = jnp.zeros((8, out_cols), F32)
    for half in range(2):
        spread = dot(parts, one_hot_columns(128, half * 64 + lane // taps))
        hit = sub * 2 + half == slot
        total = total + jnp.where(hit, spread[0:8] + spread[8:16] + spread[16:24], 0.0)
    return jnp.sum(total, axis=0, keepdims=True)


def finish(dims, feat_in, row_a, row_b, bias, out_feat, out_gw, out_gb, sem):
    n_y, n_z = dims
    rows_own = CH // (2 * n_y * n_z)
    copy = pltpu.make_async_copy(feat_in, out_feat, sem)
    copy.start()
    scale = 1.0 / math.sqrt(4 * n_y * n_z * PATCHES * 2 * CELLS)
    for r in range(rows_own):
        out_gw[r : r + 1, 0:1024] = (
            pick(row_b[r : r + 1], 8, 1024, 16, lambda t: t) * scale
        )
        out_gw[r : r + 1, 1024:1600] = (
            pick(row_a[r : r + 1], 6, 576, 9, lambda t: t // 3 * 4 + t % 3) * scale
        )
    out_gb[...] = bias[:, 0:CH] * (1.0 / math.sqrt(2 * PATCHES * CELLS))
    copy.wait()


def grid_of(scenes):
    n_z = 8 if scenes == 128 else 1
    return scenes // (4 * n_z), n_z


def local(dims, features_in, sw, dw, tb, cot, fp, vc, to):
    n_y, n_z = dims
    rows_own = CH // (2 * n_y * n_z)
    rows_y = 2 * rows_own * n_z
    vmem = pl.BlockSpec(memory_space=pltpu.VMEM)
    hbm = pl.BlockSpec(memory_space=pltpu.HBM)
    anywhere = pl.BlockSpec(memory_space=pl.ANY)
    dma = pltpu.SemaphoreType.DMA
    V = pltpu.VMEM
    pairs = [
        (lambda c: V((CH, c), F32)),
        (lambda c: V((CH, c), BF16)),
        (lambda c: V((n_y, rows_y, c), BF16)),
        (lambda c: V((n_z, 2 * rows_own, c), BF16)),
        (lambda c: V((n_z, 2 * rows_own, c), BF16)),
        (lambda c: V((2, rows_own, c), F32)),
        (lambda c: V((4, rows_own, c), F32)),
    ]
    feat, row_a, row_b, bias = pl.pallas_call(
        functools.partial(kernel, dims),
        out_shape=(
            jax.ShapeDtypeStruct(features_in.shape, BF16),
            jax.ShapeDtypeStruct((rows_own, COLS[0]), F32),
            jax.ShapeDtypeStruct((rows_own, COLS[1]), F32),
            jax.ShapeDtypeStruct((1, 128), F32),
        ),
        in_specs=[hbm] * 8,
        out_specs=(anywhere, vmem, vmem, vmem),
        scratch_shapes=[
            V((CH, 1024), BF16),
            V((CH, 576), BF16),
            V(tb.shape[::-1], F32),
            V((PATCHES, CELLS), BF16),
            pltpu.SMEM(fp.shape[::-1], jnp.int32),
            pltpu.SMEM(vc.shape, jnp.int32),
            pltpu.SMEM(to.shape, jnp.int32),
            V((PATCHES, GROUPS, CH, GROUP), BF16),
            V((GROUP, 1024), BF16),
            V((1024, 1024), BF16),
            V((576, 768), BF16),
            V((256, 256), BF16),
            V((192, 192), BF16),
            V((PATCHES, 512, CELLS), BF16),
            V((PATCHES, CH, CELLS), F32),
            V((PATCHES, 192, CELLS), BF16),
            V((PATCHES, CH, CELLS), BF16),
            V((4, CH, CELLS), BF16),
            V((2, 2, CELLS), BF16),
            V((PATCHES, 192, CELLS), BF16),
            V((PATCHES, 256, CELLS), BF16),
            *[make(c) for make in pairs for c in COLS],
            V((1, 128), F32),
            V((n_y, 1, 128), F32),
            V((n_z, n_y, 1, 128), F32),
            V((8, 1, 128), F32),
            V((8, 1, 128), F32),
            V((GROUPS * CH, 1024), BF16),
            V((PATCHES, CH, 4096), BF16),
            dma((7,)),
            dma((PATCHES, GROUPS)),
            dma((PATCHES,)),
            dma((2, 3)),
            dma((2, 3)),
            dma((3, n_y)),
            dma((3, n_y)),
            dma((3, n_z)),
            dma((3, n_z)),
            dma((2, 2, 2)),
            dma((2, 4)),
            dma((8,)),
            dma((8,)),
        ],
        compiler_params=pltpu.CompilerParams(
            collective_id=0, has_side_effects=True, vmem_limit_bytes=48 * 1024 * 1024
        ),
    )(
        *(
            pltpu.with_memory_space_constraint(a, pltpu.HBM)
            for a in (features_in, sw, dw, tb.T, cot, fp.T, vc, to)
        )
    )
    return pl.pallas_call(
        functools.partial(finish, dims),
        out_shape=(
            jax.ShapeDtypeStruct(features_in.shape, BF16),
            jax.ShapeDtypeStruct((rows_own, 1600), F32),
            jax.ShapeDtypeStruct((1, CH), F32),
        ),
        in_specs=[anywhere, vmem, vmem, vmem],
        out_specs=(hbm, vmem, vmem),
        scratch_shapes=[dma],
        compiler_params=pltpu.CompilerParams(vmem_limit_bytes=16 * 1024 * 1024),
    )(feat, row_a, row_b, bias)


def solution(mesh):
    return jax.shard_map(
        functools.partial(local, grid_of(mesh.shape["scene"])),
        mesh=mesh,
        in_specs=(
            P("scene", "tile", None, None),
            P(),
            P(),
            P(),
            P("scene", "tile", None),
            P(),
            P(),
            P(),
        ),
        out_specs=(P("scene", "tile", None, None), P("scene", None), P(("scene", "tile"), None)),
        check_vma=False,
    )
```

```python
import functools
import math

import jax
import jax.numpy as jnp
from jax import lax
from jax.experimental import pallas as pl
from jax.experimental.pallas import tpu as pltpu
from jax.sharding import PartitionSpec as P

F32 = jnp.float32
BF16 = jnp.bfloat16
MESH = pl.DeviceIdType.MESH

CH = 64
SIDE = 32
CELLS = SIDE * SIDE
GROUP = 512
GROUPS = 8
COLS = (768, 1024)
PATCHES = 2


def iota(shape, dim):
    return lax.broadcasted_iota(jnp.int32, shape, dim)


def dot(a, b):
    return lax.dot_general(a, b, (((1,), (0,)), ((), ())), preferred_element_type=F32)


def dot_nt(a, b):
    return lax.dot_general(a, b, (((1,), (1,)), ((), ())), preferred_element_type=F32)


def one_hot_columns(rows, target):
    cols = target.shape[1]
    hit = iota((rows, cols), 0) == target
    return jnp.where(hit, 1.0, 0.0).astype(BF16)


def column_taps(sel):
    lane = iota((CH, 128), 1)
    column = iota((CH, 128), 0)
    zero = jnp.zeros((CH, 512), BF16)
    for tap in range(4):
        ones = jnp.where(column == 2 * (lane % SIDE) - 1 + tap, 1.0, 0.0)
        for row in range(4):
            block = jnp.where(lane // SIDE == row, ones, 0.0).astype(BF16)
            for parity in range(2):
                top = (2 * row + parity) * CH
                left = parity * 512 + tap * 128
                sel[top : top + CH, left : left + 128] = block
    for row in range(8):
        left = 512 - row % 2 * 512
        sel[row * CH : (row + 1) * CH, left : left + 512] = zero


def shift_rows(x, cells):
    lane = iota(x.shape, 1)
    moved = pltpu.roll(x, (-cells) % CELLS, 1)
    keep = lane < CELLS - cells if cells > 0 else lane >= -cells
    return jnp.where(keep, moved, 0.0)


def shift_cols(x, cells):
    col = iota(x.shape, 1) % SIDE
    moved = pltpu.roll(x, (-cells) % CELLS, 1)
    keep = col < SIDE - cells if cells > 0 else col >= -cells
    return jnp.where(keep, moved, 0.0)


def kernel(
    dims,
    feat,
    sw_in,
    dw_in,
    tb_in,
    cot_in,
    fp_in,
    vc_in,
    to_in,
    out_feat,
    out_a,
    out_b,
    out_bias,
    sw,
    dw,
    tb,
    cot,
    fp,
    vc,
    to,
    xs,
    sel,
    turned_s,
    turned_d,
    wp,
    wt,
    vp,
    vt,
    taps,
    pre,
    act3,
    mine,
    theirs,
    their_cot,
    gr,
    pr,
    gw_a,
    gw_b,
    ysend_a,
    ysend_b,
    yrecv_a,
    yrecv_b,
    zsend_a,
    zsend_b,
    zrecv_a,
    zrecv_b,
    xsend_a,
    xsend_b,
    xrecv_a,
    xrecv_b,
    bown,
    by,
    bz,
    bsend,
    brecv,
    stack,
    feat_out,
    w_sem,
    in_sem,
    out_sem,
    ex_send,
    ex_recv,
    y_send,
    y_recv,
    z_send,
    z_recv,
    x_send,
    x_recv,
    bx_send,
    bx_recv,
):
    n_y, n_z = dims
    rows_own = CH // (2 * n_y * n_z)
    rows_z = 2 * rows_own
    rows_y = rows_z * n_z
    gw = (gw_a, gw_b)
    ysend = (ysend_a, ysend_b)
    yrecv = (yrecv_a, yrecv_b)
    zsend = (zsend_a, zsend_b)
    zrecv = (zrecv_a, zrecv_b)
    xsend = (xsend_a, xsend_b)
    xrecv = (xrecv_a, xrecv_b)
    scene = lax.axis_index("scene")
    tile = lax.axis_index("tile")
    core = lax.rem(scene, 2)
    z = lax.rem(scene // 2, n_z)
    y = lax.rem(scene // (2 * n_z), n_y)
    x_lo = scene // (2 * n_z * n_y)
    pair = scene // 2

    def scene_of(xl, yy, zz, cc):
        return ((xl * n_y + yy) * n_z + zz) * 2 + cc

    def at_y(d):
        return lax.rem(y + d, n_y)

    def at_z(d):
        return lax.rem(z + d, n_z)

    def ring(k):
        return scene_of(k // 4, y, z, (k // 2) % 2), k % 2

    me_ring = x_lo * 4 + core * 2 + tile

    def other(k):
        return lax.rem(me_ring + k, 8)

    def load(p, h):
        return pltpu.make_async_copy(
            feat.at[0, p, :, pl.ds(h * GROUP, GROUP)], xs.at[p, h], in_sem.at[p, h]
        )

    def load_small(i):
        source, target = (
            (sw_in.at[core], sw),
            (dw_in.at[core], dw),
            (tb_in, tb),
            (cot_in.at[0], cot),
            (fp_in, fp),
            (vc_in, vc),
            (to_in, to),
        )[i]
        return pltpu.make_async_copy(source, target, w_sem.at[i])

    load_small(0).start()
    load_small(1).start()
    for h in range(GROUPS):
        load(0, h).start()
    for i in range(2, 7):
        load_small(i).start()
    for h in range(GROUPS):
        load(1, h).start()

    barrier = pltpu.get_barrier_semaphore()
    for d in range(1, n_y):
        pl.semaphore_signal(
            barrier, inc=1, device_id=(scene_of(x_lo, at_y(d), z, core), tile), device_id_type=MESH
        )
    for d in range(1, n_z):
        pl.semaphore_signal(
            barrier, inc=1, device_id=(scene_of(x_lo, y, at_z(d), core), tile), device_id_type=MESH
        )
    for k in range(1, 8):
        pl.semaphore_signal(barrier, inc=1, device_id=ring(other(k)), device_id_type=MESH)

    column_taps(sel)

    load_small(0).wait()
    turned_s[...] = sw[...].T.astype(F32)
    for half, rows in enumerate(((1, 3), (0, 2))):
        for col in range(4):
            block = jnp.concatenate(
                [turned_s[pl.ds(row * 4 + col, CH, stride=16), :] for row in rows], axis=1
            )
            block = block.astype(BF16)
            wt[half, col * CH : (col + 1) * CH, :] = block
            wp[half * 128 : (half + 1) * 128, col * CH : (col + 1) * CH] = block.T
    load_small(1).wait()
    turned_d[...] = dw[...].T.astype(F32)
    for col in range(3):
        block = jnp.concatenate(
            [turned_d[pl.ds(row * 3 + col, CH, stride=9), :] for row in range(3)], axis=1
        )
        block = block.astype(BF16)
        vt[col * CH : (col + 1) * CH, :] = block
        vp[:, col * CH : (col + 1) * CH] = block.T
    for i in range(2, 7):
        load_small(i).wait()
    bias = jnp.sum(jnp.where(iota(tb.shape, 1) == to[scene], tb[...], 0.0), axis=1, keepdims=True)

    def split(p):
        for h in range(GROUPS):
            load(p, h).wait()
        parts = dot(xs[p].reshape(GROUPS * CH, GROUP), sel[...]).astype(BF16)
        for h in range(GROUPS):
            for n in range(8):
                taps[p, n * CH : (n + 1) * CH, h * 128 : (h + 1) * 128] = parts[
                    h * CH : (h + 1) * CH, n * 128 : (n + 1) * 128
                ]

    def partner(to_ring):
        return scene_of(x_lo, y, z, 1 - core), tile if to_ring == 0 else 1 - tile

    def push(p, to_ring):
        return pltpu.make_async_remote_copy(
            src_ref=mine.at[p],
            dst_ref=theirs.at[tile * 2 + p],
            send_sem=ex_send.at[to_ring, p],
            recv_sem=ex_recv.at[tile, p],
            device_id=partner(to_ring),
            device_id_type=MESH,
        )

    def push_cot(to_ring):
        return pltpu.make_async_remote_copy(
            src_ref=cot,
            dst_ref=their_cot.at[tile],
            send_sem=ex_send.at[to_ring, 2],
            recv_sem=ex_recv.at[tile, 2],
            device_id=partner(to_ring),
            device_id_type=MESH,
        )

    def forward(p):
        even = dot(wp[0:128, :], taps[p, 0:256, :])
        odd = dot(wp[128:256, :], taps[p, 256:512, :])
        pre_act = (
            even[0:CH]
            + odd[CH:]
            + shift_rows(even[CH:], SIDE)
            + shift_rows(odd[0:CH], -SIDE)
            + bias
        )
        pre[p] = pre_act
        act = (pre_act * jax.nn.sigmoid(pre_act)).astype(BF16)
        wide = act.astype(F32)
        act3[p, 0:CH] = shift_cols(wide, -2).astype(BF16)
        act3[p, CH : 2 * CH] = act
        act3[p, 2 * CH :] = shift_cols(wide, 2).astype(BF16)
        rows = dot(vp[...], act3[p])
        out = (
            rows[CH : 2 * CH]
            + shift_rows(rows[0:CH], -2 * SIDE)
            + shift_rows(rows[2 * CH :], 2 * SIDE)
        )
        mine[p] = out.astype(BF16)

    for p in range(PATCHES):
        split(p)
        forward(p)
        if p == 0:
            pl.semaphore_wait(barrier, (n_y - 1) + (n_z - 1) + 7)
        for to_ring in (1, 0):
            push(p, to_ring).start()
            if p == 0:
                push_cot(to_ring).start()

    for p in range(PATCHES):
        v = pre[p]
        g = jax.nn.sigmoid(v)
        pre[p] = g * (1.0 + v * (1.0 - g))

    def pairing(j):
        inverse = jnp.int32(0)
        for i in range(4):
            inverse = jnp.where(fp[i, pair] == j, i, inverse)
        return jnp.where(core == 0, fp[j, pair], inverse)

    live_count = vc[pair]

    for t in range(2):
        for p in range(3):
            if p < 2:
                pltpu.make_async_copy(mine.at[p], theirs.at[t * 2 + p], ex_recv.at[t, p]).wait()
            else:
                pltpu.make_async_copy(cot, their_cot.at[t], ex_recv.at[t, 2]).wait()

    def y_copy(c, d):
        return pltpu.make_async_remote_copy(
            src_ref=ysend[c].at[pl.ds(pl.multiple_of(at_y(d) * rows_y, rows_y), rows_y), :],
            dst_ref=yrecv[c].at[y],
            send_sem=y_send.at[c, d],
            recv_sem=y_recv.at[c, y],
            device_id=(scene_of(x_lo, at_y(d), z, core), tile),
            device_id_type=MESH,
        )

    def by_copy(d):
        return pltpu.make_async_remote_copy(
            src_ref=bown,
            dst_ref=by.at[y],
            send_sem=y_send.at[2, d],
            recv_sem=y_recv.at[2, y],
            device_id=(scene_of(x_lo, at_y(d), z, core), tile),
            device_id_type=MESH,
        )

    def z_copy(c, d):
        return pltpu.make_async_remote_copy(
            src_ref=zsend[c].at[at_z(d)],
            dst_ref=zrecv[c].at[z],
            send_sem=z_send.at[c, d],
            recv_sem=z_recv.at[c, z],
            device_id=(scene_of(x_lo, y, at_z(d), core), tile),
            device_id_type=MESH,
        )

    def bz_copy(d):
        return pltpu.make_async_remote_copy(
            src_ref=by,
            dst_ref=bz.at[z],
            send_sem=z_send.at[2, d],
            recv_sem=z_recv.at[2, z],
            device_id=(scene_of(x_lo, y, at_z(d), core), tile),
            device_id_type=MESH,
        )

    here = tile * 2 + x_lo

    def x_copy(c, r, t):
        return pltpu.make_async_remote_copy(
            src_ref=xsend[c].at[r],
            dst_ref=xrecv[c].at[here],
            send_sem=x_send.at[c, r, t],
            recv_sem=x_recv.at[c, here],
            device_id=(scene_of(core, y, z, r), t),
            device_id_type=MESH,
        )

    def is_me(r, t):
        return (x_lo == core) & (core == r) & (tile == t)

    def bx_copy(k):
        return pltpu.make_async_remote_copy(
            src_ref=bsend.at[other(k)],
            dst_ref=brecv.at[me_ring],
            send_sem=bx_send.at[k],
            recv_sem=bx_recv.at[me_ring],
            device_id=ring(other(k)),
            device_id_type=MESH,
        )

    def start_y(c):
        ysend[c][...] = gw[c][...].astype(BF16)
        for d in range(n_y - 1, 0, -1):
            y_copy(c, d).start()

    def y_to_z(c):
        total = gw[c][pl.ds(pl.multiple_of(y * rows_y, rows_y), rows_y), :]
        for d in range(1, n_y):
            source = at_y(d)
            pltpu.make_async_copy(
                ysend[c].at[0:rows_y, :], yrecv[c].at[source], y_recv.at[c, source]
            ).wait()
            total = total + yrecv[c][source].astype(F32)
        for k in range(n_z):
            zsend[c][k] = total[k * rows_z : (k + 1) * rows_z].astype(BF16)
        for d in range(1, n_z):
            z_copy(c, d).start()

    def z_to_x(c):
        total = zsend[c][z].astype(F32)
        for d in range(1, n_z):
            source = at_z(d)
            pltpu.make_async_copy(zsend[c].at[0], zrecv[c].at[source], z_recv.at[c, source]).wait()
            total = total + zrecv[c][source].astype(F32)
        for r in range(2):
            xsend[c][r] = total[r * rows_own : (r + 1) * rows_own]
        for r in range(2):
            for t in range(2):

                @pl.when(jnp.logical_not(is_me(r, t)))
                def _():
                    x_copy(c, r, t).start()

                @pl.when(is_me(r, t))
                def _():
                    xrecv[c][pl.ds(here, 1)] = xsend[c][r][None]

    def x_done(c, out):
        for s in range(4):

            @pl.when(jnp.logical_not((core == x_lo) & (here == s)))
            def _():
                pltpu.make_async_copy(xsend[c].at[0], xrecv[c].at[s], x_recv.at[c, s]).wait()

        out[...] = xrecv[c][0] + xrecv[c][1] + xrecv[c][2] + xrecv[c][3]

    for p in range(PATCHES):
        j = tile * PATCHES + p
        matched = pairing(j)
        partner_cot = jnp.zeros((1, CELLS), F32)
        for t in range(2):
            both = their_cot[t].astype(F32)
            for i in range(2):
                partner_cot = partner_cot + jnp.where(matched == t * 2 + i, both[i : i + 1], 0.0)
        own_cot = cot[...].astype(F32)[p : p + 1]
        live = jnp.where(j < live_count, 1.0, 0.0).astype(F32)
        signal = (own_cot + partner_cot) * live
        out_grad = (signal * theirs[matched].astype(F32)).astype(BF16)
        wide = out_grad.astype(F32)
        gr[p, 0:CH] = shift_rows(wide, 2 * SIDE).astype(BF16)
        gr[p, CH : 2 * CH] = out_grad
        gr[p, 2 * CH :] = shift_rows(wide, -2 * SIDE).astype(BF16)
        gdil = dot_nt(gr[p], act3[p])
        for tap in range(3):
            part = gdil[tap * CH : (tap + 1) * CH]
            where = slice(tap * 256, tap * 256 + 192)
            if p == 0:
                gw_a[:, where] = part
                gw_a[:, tap * 256 + 192 : (tap + 1) * 256] = jnp.zeros((CH, 64), F32)
            else:
                gw_a[:, where] += part
    start_y(0)

    bias_col = jnp.zeros((CH, 1), F32)
    for p in range(PATCHES):
        cols = dot(vt[...], gr[p])
        act_grad = (
            cols[CH : 2 * CH] + shift_cols(cols[0:CH], 2) + shift_cols(cols[2 * CH :], -2)
        )
        pre_grad = act_grad * pre[p]
        bias_col = bias_col + jnp.sum(pre_grad, axis=1, keepdims=True)
        narrow = pre_grad.astype(BF16)
        wide = narrow.astype(F32)
        pr[p, 0:CH] = narrow
        pr[p, CH : 2 * CH] = shift_rows(wide, -SIDE).astype(BF16)
        pr[p, 2 * CH : 3 * CH] = shift_rows(wide, SIDE).astype(BF16)
        pr[p, 3 * CH :] = narrow
        geven = dot_nt(pr[p, 0:128], taps[p, 0:256])
        godd = dot_nt(pr[p, 128:256], taps[p, 256:512])
        for slot, tap in enumerate((1, 3, 0, 2)):
            part = (geven if slot < 2 else godd)[(slot % 2) * CH : (slot % 2 + 1) * CH]
            where = slice(tap * 256, (tap + 1) * 256)
            if p == 0:
                gw_b[:, where] = part
            else:
                gw_b[:, where] += part
    start_y(1)

    wide_eye = iota((CH, 128), 0) == iota((CH, 128), 1)
    bown[...] = jnp.sum(
        jnp.where(wide_eye, jnp.broadcast_to(bias_col, (CH, 128)), 0.0), axis=0, keepdims=True
    )
    for d in range(1, n_y):
        by_copy(d).start()
    by[pl.ds(y, 1)] = bown[...][None]

    def store(p):
        return pltpu.make_async_copy(feat_out.at[p], out_feat.at[0, p], out_sem.at[p])

    def feature_grad(p):
        for half in range(2):
            part = dot(wt[half], pr[p, half * 128 : (half + 1) * 128, :]).astype(BF16)
            for h in range(GROUPS):
                for n in range(4):
                    stack[h * CH : (h + 1) * CH, (half * 4 + n) * 128 : (half * 4 + n + 1) * 128] = (
                        part[n * CH : (n + 1) * CH, h * 128 : (h + 1) * 128]
                    )
        whole = dot_nt(stack[...], sel[...]).astype(BF16)
        for h in range(GROUPS):
            feat_out[p, :, h * GROUP : (h + 1) * GROUP] = whole[h * CH : (h + 1) * CH]
        store(p).start()

    feature_grad(0)
    y_to_z(0)
    feature_grad(1)
    y_to_z(1)
    for d in range(1, n_y):
        source = at_y(d)
        pltpu.make_async_copy(bown, by.at[source], y_recv.at[2, source]).wait()
    for d in range(1, n_z):
        bz_copy(d).start()
    z_to_x(0)
    z_to_x(1)

    bz[pl.ds(z, 1)] = by[...][None]
    for d in range(1, n_z):
        source = at_z(d)
        pltpu.make_async_copy(by, bz.at[source], z_recv.at[2, source]).wait()
    k8 = iota((8, 128), 0)
    tile_ids = scene_of(k8 // 4, y, z, (k8 // 2) % 2) * 2 + k8 % 2
    sums = jnp.zeros((8, 128), F32)
    for zz in range(n_z):
        for yy in range(n_y):
            owner = to[scene_of(x_lo, yy, zz, core)]
            sums = sums + jnp.where(tile_ids == owner, bz[zz, yy], 0.0)
    for k in range(8):
        bsend[k] = sums[k : k + 1]
    for k in range(1, 8):
        bx_copy(k).start()
    brecv[pl.ds(me_ring, 1)] = bsend[pl.ds(me_ring, 1)]

    x_done(0, out_a)
    x_done(1, out_b)
    for k in range(1, 8):
        source = other(k)
        pltpu.make_async_copy(bsend.at[0], brecv.at[source], bx_recv.at[source]).wait()
    bias_total = brecv[0]
    for k in range(1, 8):
        bias_total = bias_total + brecv[k]
    out_bias[...] = bias_total

    for p in range(PATCHES):
        store(p).wait()
    for to_ring in range(2):
        push_cot(to_ring).wait_send()
        for p in range(PATCHES):
            push(p, to_ring).wait_send()
    for d in range(1, n_y):
        for c in range(2):
            y_copy(c, d).wait_send()
        by_copy(d).wait_send()
    for d in range(1, n_z):
        for c in range(2):
            z_copy(c, d).wait_send()
        bz_copy(d).wait_send()
    for c in range(2):
        for r in range(2):
            for t in range(2):

                @pl.when(jnp.logical_not(is_me(r, t)))
                def _():
                    x_copy(c, r, t).wait_send()

    for k in range(1, 8):
        bx_copy(k).wait_send()


def pick(row, vregs, out_cols, taps, slot_of):
    split = jnp.concatenate([row[:, q * 128 : (q + 1) * 128] for q in range(vregs)], axis=0)
    if vregs < 8:
        split = jnp.concatenate([split, jnp.zeros((8 - vregs, 128), F32)], axis=0)
    high = split.astype(BF16).astype(F32)
    rest = split - high
    middle = rest.astype(BF16).astype(F32)
    low = rest - middle
    parts = jnp.concatenate([high, middle, low], axis=0).astype(BF16)
    lane = iota((1, out_cols), 1)
    slot = slot_of(lane % taps)
    sub = iota((8, out_cols), 0)
    total = jnp.zeros((8, out_cols), F32)
    for half in range(2):
        spread = dot(parts, one_hot_columns(128, half * 64 + lane // taps))
        hit = sub * 2 + half == slot
        total = total + jnp.where(hit, spread[0:8] + spread[8:16] + spread[16:24], 0.0)
    return jnp.sum(total, axis=0, keepdims=True)


def finish(dims, feat_in, row_a, row_b, bias, out_feat, out_gw, out_gb, sem):
    n_y, n_z = dims
    rows_own = CH // (2 * n_y * n_z)
    copy = pltpu.make_async_copy(feat_in, out_feat, sem)
    copy.start()
    scale = 1.0 / math.sqrt(4 * n_y * n_z * PATCHES * 2 * CELLS)
    for r in range(rows_own):
        out_gw[r : r + 1, 0:1024] = (
            pick(row_b[r : r + 1], 8, 1024, 16, lambda t: t) * scale
        )
        out_gw[r : r + 1, 1024:1600] = (
            pick(row_a[r : r + 1], 6, 576, 9, lambda t: t // 3 * 4 + t % 3) * scale
        )
    out_gb[...] = bias[:, 0:CH] * (1.0 / math.sqrt(2 * PATCHES * CELLS))
    copy.wait()


def grid_of(scenes):
    n_z = 8 if scenes == 128 else 1
    return scenes // (4 * n_z), n_z


def local(dims, features_in, sw, dw, tb, cot, fp, vc, to):
    n_y, n_z = dims
    rows_own = CH // (2 * n_y * n_z)
    rows_y = 2 * rows_own * n_z
    vmem = pl.BlockSpec(memory_space=pltpu.VMEM)
    hbm = pl.BlockSpec(memory_space=pltpu.HBM)
    anywhere = pl.BlockSpec(memory_space=pl.ANY)
    dma = pltpu.SemaphoreType.DMA
    V = pltpu.VMEM
    pairs = [
        (lambda c: V((CH, c), F32)),
        (lambda c: V((CH, c), BF16)),
        (lambda c: V((n_y, rows_y, c), BF16)),
        (lambda c: V((n_z, 2 * rows_own, c), BF16)),
        (lambda c: V((n_z, 2 * rows_own, c), BF16)),
        (lambda c: V((2, rows_own, c), F32)),
        (lambda c: V((4, rows_own, c), F32)),
    ]
    feat, row_a, row_b, bias = pl.pallas_call(
        functools.partial(kernel, dims),
        out_shape=(
            jax.ShapeDtypeStruct(features_in.shape, BF16),
            jax.ShapeDtypeStruct((rows_own, COLS[0]), F32),
            jax.ShapeDtypeStruct((rows_own, COLS[1]), F32),
            jax.ShapeDtypeStruct((1, 128), F32),
        ),
        in_specs=[hbm] * 8,
        out_specs=(anywhere, vmem, vmem, vmem),
        scratch_shapes=[
            V((CH, 1024), BF16),
            V((CH, 576), BF16),
            V(tb.shape[::-1], F32),
            V((PATCHES, CELLS), BF16),
            pltpu.SMEM(fp.shape[::-1], jnp.int32),
            pltpu.SMEM(vc.shape, jnp.int32),
            pltpu.SMEM(to.shape, jnp.int32),
            V((PATCHES, GROUPS, CH, GROUP), BF16),
            V((GROUP, 1024), BF16),
            V((1024, CH), F32),
            V((576, CH), F32),
            V((256, 256), BF16),
            V((2, 256, 128), BF16),
            V((192, 192), BF16),
            V((192, 192), BF16),
            V((PATCHES, 512, CELLS), BF16),
            V((PATCHES, CH, CELLS), F32),
            V((PATCHES, 192, CELLS), BF16),
            V((PATCHES, CH, CELLS), BF16),
            V((4, CH, CELLS), BF16),
            V((2, 2, CELLS), BF16),
            V((PATCHES, 192, CELLS), BF16),
            V((PATCHES, 256, CELLS), BF16),
            *[make(c) for make in pairs for c in COLS],
            V((1, 128), F32),
            V((n_y, 1, 128), F32),
            V((n_z, n_y, 1, 128), F32),
            V((8, 1, 128), F32),
            V((8, 1, 128), F32),
            V((GROUPS * CH, 1024), BF16),
            V((PATCHES, CH, 4096), BF16),
            dma((7,)),
            dma((PATCHES, GROUPS)),
            dma((PATCHES,)),
            dma((2, 3)),
            dma((2, 3)),
            dma((3, n_y)),
            dma((3, n_y)),
            dma((3, n_z)),
            dma((3, n_z)),
            dma((2, 2, 2)),
            dma((2, 4)),
            dma((8,)),
            dma((8,)),
        ],
        compiler_params=pltpu.CompilerParams(
            collective_id=0, has_side_effects=True, vmem_limit_bytes=48 * 1024 * 1024
        ),
    )(
        *(
            pltpu.with_memory_space_constraint(a, pltpu.HBM)
            for a in (features_in, sw, dw, tb.T, cot, fp.T, vc, to)
        )
    )
    return pl.pallas_call(
        functools.partial(finish, dims),
        out_shape=(
            jax.ShapeDtypeStruct(features_in.shape, BF16),
            jax.ShapeDtypeStruct((rows_own, 1600), F32),
            jax.ShapeDtypeStruct((1, CH), F32),
        ),
        in_specs=[anywhere, vmem, vmem, vmem],
        out_specs=(hbm, vmem, vmem),
        scratch_shapes=[dma],
        compiler_params=pltpu.CompilerParams(vmem_limit_bytes=16 * 1024 * 1024),
    )(feat, row_a, row_b, bias)


def solution(mesh):
    return jax.shard_map(
        functools.partial(local, grid_of(mesh.shape["scene"])),
        mesh=mesh,
        in_specs=(
            P("scene", "tile", None, None),
            P(),
            P(),
            P(),
            P("scene", "tile", None),
            P(),
            P(),
            P(),
        ),
        out_specs=(P("scene", "tile", None, None), P("scene", None), P(("scene", "tile"), None)),
        check_vma=False,
    )
```
